32 devices in a mesh: snap: 4 (over y, x), height: 8 (over z, core).
Axes of the slice: x: 2, y: 2, z: 4, core: 2. Of those that a mesh axis runs over, the one named last changes fastest.
Arguments:
- resolved: bfloat16 [64, 3, 128, 16, 2, 128], P('snap', None, 'height'), may hold values from -6 to 6
- drain: bfloat16 [64, 3, 128, 16, 2, 128], P('snap', None, 'height'), may hold values from -6 to 6
- pair_list: int32 [64, 2], replicated, may hold values from 0 to 127, as said below
- ridge_index: int32 [64], replicated, may hold values from 0 to 3
Outputs:
- predicted: float32 [64, 3, 128, 2, 64], P('snap', None, 'height')
- misfit: float32 [1], replicated
The draws below stay inside these ranges and needn't reach their ends.
Inputs may be any that keep to these rules, and one draw needn't show every extreme that they name: `pair_list`: each row names a streamwise mode below 16 and a spanwise wavenumber below 128; no row repeats.
All inputs are finite; a program needn't handle non-finite values.
Results may differ from the reference program's by a relative error of at most 0.0032.
Values sent between devices are 32-bit elements; how exact they have to be, the bound alone decides.
A program may use at most 128 MiB of HBM per device.

```python
import math
import jax
import jax.numpy as jnp
from jax import lax

Z = 128
KX = 16
H = 128
C = 3
S = 64
PAIRS = 64


def draw_pair_list(key, part):
    total = KX * Z
    first = jax.random.permutation(jax.random.fold_in(key, 11), total - 1)[:PAIRS - 1].astype(jnp.int32)
    chosen = jnp.concatenate([first, jnp.full((1,), total - 1, jnp.int32)])
    order = jax.random.permutation(jax.random.fold_in(key, 12), PAIRS)
    chosen = chosen[order]
    return jnp.stack([chosen // Z, chosen % Z], axis=1).astype(jnp.int32)


def plant(entries, stream_key, least, high):
    place = [jax.random.randint(jax.random.fold_in(stream_key, axis), (), 0, length) for axis, length in enumerate(entries.shape)]
    longest = entries.shape.index(max(entries.shape))
    neighbour = place[:longest] + [(place[longest] + 1) % entries.shape[longest]] + place[longest + 1:]
    return entries.at[tuple(place)].set(least).at[tuple(neighbour)].set(high)


def shard_levels(rng, dims, shards, least, largest):
    def one(position, parts):
        heights = jax.random.uniform(jax.random.fold_in(jax.random.fold_in(rng, 6), position), (parts,), jnp.float32, least / len(shards), largest / len(shards))
        return jnp.repeat(jnp.exp(heights), dims[position] // parts).reshape((-1,) + (1,) * (len(dims) - position - 1))

    level = one(*shards[0])
    for cut in shards[1:]:
        level = level * one(*cut)
    return level


def bell_draw(stream_key, extent, scale, limit, split=(), held_as=jnp.bfloat16):
    level = shard_levels(stream_key, extent, split, -0.22, 0.18) if split else 1.0
    drawn = jax.random.normal(stream_key, extent, jnp.float32) * scale * level
    return jnp.minimum(jnp.maximum(drawn, -limit), limit).astype(held_as)


def setup_inputs(seed: int = 0) -> dict:
    keys = jax.random.split(jax.random.key(seed), 5)
    return {
        "resolved": bell_draw(keys[0], (S, C, H, KX, 2, Z), 1.0, 6.0, ((0, 4), (2, 8))),
        "drain": bell_draw(keys[1], (S, C, H, KX, 2, Z), 1.0, 6.0, ((0, 4), (2, 8))),
        "pair_list": draw_pair_list(jax.random.fold_in(keys[4], 71), 0),
        "ridge_index": plant(jax.random.randint(keys[3], (PAIRS,), 0, 4), jax.random.fold_in(keys[3], 1), 0, 3).astype(jnp.int32),
    }


def twiddles(length):
    grid = jnp.arange(length, dtype=jnp.int32)
    phase = grid[:, None] * grid[None, :] % length
    theta = phase.astype(jnp.float32) * (2.0 * math.pi / length)
    scaling = 1.0 / math.sqrt(length)
    cosine = jnp.cos(theta) * scaling
    sine = jnp.sin(theta) * scaling
    upper = jnp.concatenate([cosine, -sine], axis=1)
    lower = jnp.concatenate([sine, cosine], axis=1)
    return jnp.concatenate([upper, lower], axis=0).astype(jnp.bfloat16)

def spectrum_at(values, entry, twiddle):
    mode_rows = jnp.take(values, entry[0], axis=3)
    picked = jnp.stack([jnp.take(twiddle, entry[1], axis=1), jnp.take(twiddle, entry[1] + Z, axis=1)], axis=1)
    spectral = jnp.dot(mode_rows.reshape(-1, 2 * Z).astype(jnp.float32), picked.astype(jnp.float32), preferred_element_type=jnp.float32)
    return spectral.reshape(S, C * H, 2)

def reference(resolved, drain, pair_list, ridge_index):
    twiddle = twiddles(Z)
    features = C * H
    identity_matrix = jnp.eye(2 * features, dtype=jnp.float32)
    highest = lax.Precision.HIGHEST

    def one_pair(packed):
        entry, level = packed
        ridge = 0.25 * jnp.exp2(level.astype(jnp.float32))
        spec_x = spectrum_at(resolved, entry, twiddle)
        spec_y = spectrum_at(drain, entry, twiddle)
        real_x = spec_x[:, :, 0]
        imag_x = spec_x[:, :, 1]
        stacked_x = jnp.concatenate([jnp.concatenate([real_x, imag_x], 1), jnp.concatenate([-imag_x, real_x], 1)], 0)
        stacked_y = jnp.concatenate([spec_y[:, :, 0], spec_y[:, :, 1]], 0)
        gram = jnp.dot(stacked_x.T.astype(jnp.float32), stacked_x.astype(jnp.float32), precision=highest, preferred_element_type=jnp.float32) / S + ridge * identity_matrix
        moments = jnp.dot(stacked_x.T.astype(jnp.float32), stacked_y.astype(jnp.float32), precision=highest, preferred_element_type=jnp.float32) / S
        factor = jnp.linalg.cholesky(gram)
        halfway = lax.linalg.triangular_solve(factor, moments, left_side=True, lower=True, transpose_a=False)
        weights = lax.linalg.triangular_solve(factor, halfway, left_side=True, lower=True, transpose_a=True)
        fitted = jnp.dot(stacked_x.astype(jnp.float32), weights.astype(jnp.float32), precision=highest, preferred_element_type=jnp.float32)
        misses = jnp.sum((stacked_y - fitted) ** 2)
        energy = jnp.sum(stacked_y ** 2)
        return (fitted.reshape(2, S, C, H), misses, energy)
    fitted_all, misses_all, energy_all = lax.map(one_pair, (pair_list, ridge_index))
    predicted = jnp.transpose(fitted_all, (2, 3, 4, 1, 0))
    misfit = (jnp.sum(misses_all) / jnp.sum(energy_all)).reshape(1)
    return (predicted, misfit)
```

```python
import math

import jax
import jax.numpy as jnp
from jax import lax
from jax.experimental import pallas as pl
from jax.experimental.pallas import tpu as pltpu
from jax.sharding import PartitionSpec as P

HIGHEST = lax.Precision.HIGHEST
CHUNK = 8


def pair_tables(pair_list, points, mode_count):
    grid = jnp.arange(points, dtype=jnp.int32)
    phase = grid[:, None] * pair_list[None, :, 1] % points
    theta = phase.astype(jnp.float32) * (2.0 * math.pi / points)
    scaling = 1.0 / math.sqrt(points)
    cosine = jnp.cos(theta) * scaling
    sine = jnp.sin(theta) * scaling
    table = jnp.concatenate([cosine, -sine, sine, cosine], axis=1).astype(jnp.bfloat16)
    lines = jnp.arange(2 * mode_count, dtype=jnp.int32)
    chosen = (lines[:, None] // 2) == pair_list[None, :, 0]
    even = (lines % 2 == 0)[:, None]
    mask = jnp.concatenate([chosen & even, chosen & even, chosen & ~even, chosen & ~even], axis=1)
    return table, mask.astype(jnp.float32)


def spectrum_kernel(x_ref, y_ref, table_ref, mask_ref, sx_ref, sy_ref, held):
    block, lines, points = x_ref.shape
    columns = sx_ref.shape[0]
    for source, target in ((x_ref, sx_ref), (y_ref, sy_ref)):
        for start in range(0, block, CHUNK):
            rows = source[start:start + CHUNK].reshape(CHUNK * lines, points)
            product = jnp.dot(rows, table_ref[...], preferred_element_type=jnp.float32)
            product = product.reshape(CHUNK, lines, 2 * columns) * mask_ref[...][None]
            both = product[:, :, :columns] + product[:, :, columns:]
            held[start:start + CHUNK, :] = jnp.sum(both, axis=1)
        target[...] = held[...].T


def spectra(resolved, drain, pair_list):
    points = resolved.shape[-1]
    mode_count = resolved.shape[3]
    lines = 2 * mode_count
    rows = resolved.shape[0] * resolved.shape[1] * resolved.shape[2]
    columns = 2 * pair_list.shape[0]
    table, mask = pair_tables(pair_list, points, mode_count)
    block = 128
    data = pl.BlockSpec((block, lines, points), lambda i: (i, 0, 0))
    out = pl.BlockSpec((columns, block), lambda i: (0, i))
    shape = jax.ShapeDtypeStruct((columns, rows), jnp.float32)
    return pl.pallas_call(
        spectrum_kernel,
        grid=(rows // block,),
        in_specs=[data, data, pl.BlockSpec(table.shape, lambda i: (0, 0)),
                  pl.BlockSpec(mask.shape, lambda i: (0, 0))],
        out_specs=[out, out],
        out_shape=[shape, shape],
        scratch_shapes=[pltpu.VMEM((block, columns), jnp.float32)],
    )(resolved.reshape(rows, lines, points), drain.reshape(rows, lines, points), table, mask)


def solve_kernel(ridge_ref, x_ref, y_ref, fitted_ref, totals_ref):
    pairs, _, snaps, features = x_ref.shape
    lane = lax.broadcasted_iota(jnp.int32, (snaps, 2 * snaps), 1)
    line = lax.broadcasted_iota(jnp.int32, (snaps, 2 * snaps), 0)
    sign = jnp.where(lax.broadcasted_iota(jnp.int32, (1, 2 * snaps), 1) < snaps, -1.0, 1.0)

    def outer(a, b):
        return lax.dot_general(a, b, (((1,), (1,)), ((), ())), precision=HIGHEST,
                               preferred_element_type=jnp.float32)

    grams = []
    states = []
    for pair in range(pairs):
        real = x_ref[pair, 0]
        imag = x_ref[pair, 1]
        upper = jnp.concatenate([real, imag], axis=1)
        lower = jnp.concatenate([-imag, real], axis=1)
        stacked = jnp.concatenate([upper, lower], axis=0)
        gram = outer(stacked, stacked)
        grams.append(gram)
        states.append(gram[:snaps] + jnp.where(line == lane, ridge_ref[pair], 0.0))
    for k in range(snaps):
        for pair in range(pairs):
            state = states[pair]
            first = state[:, k:k + 1]
            second = state[:, snaps + k:snaps + k + 1]
            inverse = 1.0 / state[k:k + 1, k:k + 1]
            cleared = jnp.where((lane == k) | (lane == snaps + k), jnp.where((line == k) & (lane == k), 1.0, 0.0), state)
            row = cleared[k:k + 1, :] * inverse
            turned = pltpu.roll(row, snaps, 1) * sign
            states[pair] = jnp.where(line == k, row, cleared - (first * row + second * turned))
    misses = jnp.zeros((1, 1), jnp.float32)
    energy = jnp.zeros((1, 1), jnp.float32)
    for pair in range(pairs):
        top = states[pair]
        bottom = pltpu.roll(top, snaps, 1) * sign
        full = jnp.concatenate([top, bottom], axis=0)
        target = y_ref[pair].reshape(2 * snaps, features)
        inner = jnp.dot(full, target, precision=HIGHEST, preferred_element_type=jnp.float32)
        fitted = jnp.dot(grams[pair], inner, precision=HIGHEST, preferred_element_type=jnp.float32)
        fitted_ref[pair] = fitted.reshape(2, snaps, features)
        gap = target - fitted
        misses = misses + jnp.sum(gap * gap, keepdims=True)
        energy = energy + jnp.sum(target * target, keepdims=True)
    where = lax.broadcasted_iota(jnp.int32, totals_ref.shape, 0)
    totals_ref[...] = jnp.where(where == 0, misses, energy)


def per_device(resolved, drain, pair_list, ridge_index):
    snap_local, components, height_local, mode_count, halves, points = resolved.shape
    snap_count = lax.axis_size("snap")
    height_count = lax.axis_size("height")
    owners = snap_count * height_count
    pair_total = pair_list.shape[0]
    pair_local = pair_total // owners
    rows = snap_local * components * height_local
    near = components * height_local
    snaps = snap_count * snap_local
    features = height_count * near

    spec_x, spec_y = spectra(resolved, drain, pair_list)
    spec = jnp.stack([spec_x, spec_y]).reshape(2, 2, owners, pair_local, rows)
    outgoing = jnp.transpose(spec, (2, 0, 3, 1, 4))
    arrived = lax.all_to_all(outgoing, ("snap", "height"), split_axis=0, concat_axis=0, tiled=True)
    arrived = arrived.reshape(snap_count, height_count, 2, pair_local, 2, snap_local, near)
    owned = jnp.transpose(arrived, (2, 3, 4, 0, 5, 1, 6)).reshape(2, pair_local, 2, snaps, features)
    owner_index = lax.axis_index("snap") * height_count + lax.axis_index("height")
    levels = lax.dynamic_slice_in_dim(ridge_index, owner_index * pair_local, pair_local, 0)
    ridge = 0.25 * jnp.exp2(levels.astype(jnp.float32)) * snaps
    fitted, totals = pl.pallas_call(
        solve_kernel,
        in_specs=[pl.BlockSpec(memory_space=pltpu.SMEM), pl.BlockSpec(memory_space=pltpu.VMEM),
                  pl.BlockSpec(memory_space=pltpu.VMEM)],
        out_specs=[pl.BlockSpec(memory_space=pltpu.VMEM), pl.BlockSpec(memory_space=pltpu.VMEM)],
        out_shape=[jax.ShapeDtypeStruct((pair_local, 2, snaps, features), jnp.float32),
                   jax.ShapeDtypeStruct((8, 128), jnp.float32)],
    )(ridge, owned[0], owned[1])
    sums = lax.psum(totals[:2, 0], ("snap", "height"))
    misfit = (sums[0] / sums[1]).reshape(1)
    back = fitted.reshape(pair_local, 2, snap_count, snap_local, height_count, near)
    back = jnp.transpose(back, (2, 4, 0, 1, 3, 5)).reshape(owners, pair_local, 2, rows)
    returned = lax.all_to_all(back, ("snap", "height"), split_axis=0, concat_axis=0, tiled=True)
    predicted = jnp.transpose(returned, (3, 2, 0, 1)).reshape(
        snap_local, components, height_local, 2, pair_total
    )
    return (predicted, misfit)


def solution(mesh):
    return jax.shard_map(
        per_device,
        mesh=mesh,
        in_specs=(
            P("snap", None, "height", None, None, None),
            P("snap", None, "height", None, None, None),
            P(),
            P(),
        ),
        out_specs=(P("snap", None, "height", None, None), P()),
        check_vma=False,
    )
```

```python
import functools
import math

import jax
import jax.numpy as jnp
from jax import lax
from jax.experimental import pallas as pl
from jax.experimental.pallas import tpu as pltpu
from jax.sharding import PartitionSpec as P

HIGHEST = lax.Precision.HIGHEST
CHUNK = 8
LANES = 128


def pair_tables(pair_list, points, mode_count):
    grid = jnp.arange(points, dtype=jnp.int32)
    ordered = jnp.repeat(pair_list, 2, axis=0)
    imaginary = (jnp.arange(ordered.shape[0], dtype=jnp.int32) % 2 == 1)[None, :]
    phase = grid[:, None] * ordered[None, :, 1] % points
    theta = phase.astype(jnp.float32) * (2.0 * math.pi / points)
    scaling = 1.0 / math.sqrt(points)
    cosine = jnp.cos(theta) * scaling
    sine = jnp.sin(theta) * scaling
    table = jnp.concatenate(
        [jnp.where(imaginary, -sine, cosine), jnp.where(imaginary, cosine, sine)], axis=1
    ).astype(jnp.bfloat16)
    lines = jnp.arange(2 * mode_count, dtype=jnp.int32)
    chosen = (lines[:, None] // 2) == ordered[None, :, 0]
    even = (lines % 2 == 0)[:, None]
    mask = jnp.concatenate([chosen & even, chosen & ~even], axis=1)
    return table, mask.astype(jnp.float32)


def group_size(snap_local, near):
    group = 1
    while snap_local % (2 * group) == 0 and 2 * group * near <= LANES - 2:
        group *= 2
    return group


def spectrum_kernel(x_ref, table_ref, mask_ref, out_ref, held):
    block, lines, points = x_ref.shape
    columns = out_ref.shape[0]
    held[...] = jnp.zeros_like(held)
    for start in range(0, block, CHUNK):
        rows = x_ref[start:start + CHUNK].reshape(CHUNK * lines, points)
        product = jnp.dot(rows, table_ref[...], preferred_element_type=jnp.float32)
        product = product.reshape(CHUNK, lines, 2 * columns) * mask_ref[...][None]
        both = product[:, :, :columns] + product[:, :, columns:]
        held[start:start + CHUNK, :] = jnp.sum(both, axis=1)
    out_ref[:, pl.ds(pl.program_id(0), 1), :] = held[...].T[:, None, :]


def spectrum(values, table, mask, near, group):
    lines, points = values.shape[1:]
    columns = mask.shape[1] // 2
    block = near * group
    steps = values.shape[0] // block
    return pl.pallas_call(
        spectrum_kernel,
        grid=(steps,),
        in_specs=[pl.BlockSpec((block, lines, points), lambda i: (i, 0, 0)),
                  pl.BlockSpec(table.shape, lambda i: (0, 0)),
                  pl.BlockSpec(mask.shape, lambda i: (0, 0))],
        out_specs=pl.BlockSpec((columns, steps, LANES), lambda i: (0, 0, 0)),
        out_shape=jax.ShapeDtypeStruct((columns, steps, LANES), jnp.float32),
        scratch_shapes=[pltpu.VMEM((LANES, columns), jnp.float32)],
        cost_estimate=pl.CostEstimate(flops=4 * values.size * columns, bytes_accessed=2 * values.size, transcendentals=0),
    )(values, table, mask)


def gather_pair(ref, pair, near, group):
    snap_count, height_count, _, _, steps, _ = ref.shape
    lane = lax.broadcasted_iota(jnp.int32, (1, LANES), 1)
    pieces = []
    for height in range(height_count):
        parts = []
        for half in range(2):
            block = ref[:, height, pair, half].reshape(snap_count * steps, LANES)
            for member in range(group):
                moved = block if member == 0 else pltpu.roll(block, LANES - member * near, 1)
                parts.append(jnp.where(lane < near, moved, 0.0))
        pieces.append(jnp.concatenate(parts, axis=0))
    return jnp.concatenate(pieces, axis=1)


def invert_kernel(near, group, ridge_ref, x_ref, smooth_ref):
    pairs = x_ref.shape[2]
    snaps = smooth_ref.shape[1] // 2
    lane = lax.broadcasted_iota(jnp.int32, (snaps, 2 * snaps), 1)
    line = lax.broadcasted_iota(jnp.int32, (snaps, 2 * snaps), 0)
    sign = jnp.where(lax.broadcasted_iota(jnp.int32, (1, 2 * snaps), 1) < snaps, -1.0, 1.0)

    def embed(top):
        return jnp.concatenate([top, pltpu.roll(top, snaps, 1) * sign], axis=0)

    grams = []
    states = []
    for pair in range(pairs):
        stacked = gather_pair(x_ref, pair, near, group)
        gram = lax.dot_general(stacked, stacked, (((1,), (1,)), ((), ())), precision=HIGHEST,
                               preferred_element_type=jnp.float32)
        swapped = pltpu.roll(gram[snaps:], snaps, 1)
        top = gram[:snaps] + jnp.where(lane < snaps, swapped, 0.0)
        top = jnp.where(lane < snaps, top, swapped - gram[:snaps])
        grams.append(top)
        states.append(top + jnp.where(line == lane, ridge_ref[pair], 0.0))
    for k in range(snaps):
        for pair in range(pairs):
            state = states[pair]
            first = state[:, k:k + 1]
            second = state[:, snaps + k:snaps + k + 1]
            inverse = 1.0 / state[k:k + 1, k:k + 1]
            cleared = jnp.where((lane == k) | (lane == snaps + k), jnp.where((line == k) & (lane == k), 1.0, 0.0), state)
            row = cleared[k:k + 1, :] * inverse
            turned = pltpu.roll(row, snaps, 1) * sign
            states[pair] = jnp.where(line == k, row, cleared - (first * row + second * turned))
    for pair in range(pairs):
        smooth_ref[pair] = jnp.dot(embed(grams[pair]), embed(states[pair]), precision=HIGHEST,
                                   preferred_element_type=jnp.float32)


def apply_kernel(near, group, smooth_ref, y_ref, back_ref):
    snap_count, height_count, pairs, _, steps, _ = y_ref.shape
    members = snap_count * steps
    half_rows = group * members
    lane = lax.broadcasted_iota(jnp.int32, (1, LANES), 1)
    misses = jnp.zeros((1, 1), jnp.float32)
    energy = jnp.zeros((1, 1), jnp.float32)
    for pair in range(pairs):
        target = gather_pair(y_ref, pair, near, group)
        fitted = jnp.dot(smooth_ref[pair], target, precision=HIGHEST, preferred_element_type=jnp.float32)
        gap = target - fitted
        misses = misses + jnp.sum(gap * gap, keepdims=True)
        energy = energy + jnp.sum(target * target, keepdims=True)
        note = jnp.where(lane == near * group, misses, jnp.where(lane == near * group + 1, energy, 0.0))
        for height in range(height_count):
            for half in range(2):
                block = jnp.broadcast_to(note, (members, LANES))
                for member in range(group):
                    start = half * half_rows + member * members
                    piece = fitted[start:start + members, height * LANES:(height + 1) * LANES]
                    block = block + (piece if member == 0 else pltpu.roll(piece, member * near, 1))
                back_ref[:, height, pair, half] = block.reshape(snap_count, steps, LANES)


def finish_kernel(near, group, back_ref, predicted_ref, misfit_ref):
    owners, pairs, _, steps, _ = back_ref.shape
    block = near * group
    for half in range(2):
        for step in range(steps):
            sheet = back_ref[:, :, half, step, :].reshape(owners * pairs, LANES)
            predicted_ref[step * block:(step + 1) * block, half, :] = sheet.T[:block]
    notes = jnp.sum(back_ref[:, pairs - 1, 0, 0, :], axis=0, keepdims=True)
    misfit_ref[...] = notes[:, block:block + 1] / notes[:, block + 1:block + 2]


def exchange(message, number):
    return lax.all_to_all(message, ("snap", "height"), split_axis=0, concat_axis=0, tiled=True)


def per_device(resolved, drain, pair_list, ridge_index):
    snap_local, components, height_local, mode_count, halves, points = resolved.shape
    snap_count = lax.axis_size("snap")
    height_count = lax.axis_size("height")
    owners = snap_count * height_count
    pair_total = pair_list.shape[0]
    pair_local = pair_total // owners
    near = components * height_local
    rows = snap_local * near
    snaps = snap_count * snap_local
    group = group_size(snap_local, near)
    steps = snap_local // group
    sent = (owners, pair_local, 2, steps, LANES)
    held = (snap_count, height_count, pair_local, 2, steps, LANES)
    vmem = pl.BlockSpec(memory_space=pltpu.VMEM)
    smem = pl.BlockSpec(memory_space=pltpu.SMEM)

    table, mask = pair_tables(pair_list, points, mode_count)
    spec_x = spectrum(resolved.reshape(rows, -1, points), table, mask, near, group)
    arrived_x = exchange(spec_x.reshape(sent), 0)
    spec_y = spectrum(drain.reshape(rows, -1, points), table, mask, near, group)
    arrived_y = exchange(spec_y.reshape(sent), 1)
    owner_index = lax.axis_index("snap") * height_count + lax.axis_index("height")
    levels = lax.dynamic_slice_in_dim(ridge_index, owner_index * pair_local, pair_local, 0)
    ridge = 0.25 * jnp.exp2(levels.astype(jnp.float32)) * snaps
    smooth = pl.pallas_call(
        functools.partial(invert_kernel, near, group),
        in_specs=[smem, vmem],
        out_specs=vmem,
        out_shape=jax.ShapeDtypeStruct((pair_local, 2 * snaps, 2 * snaps), jnp.float32),
        cost_estimate=pl.CostEstimate(flops=10**10, bytes_accessed=2**20, transcendentals=0),
    )(ridge, arrived_x.reshape(held))
    back = pl.pallas_call(
        functools.partial(apply_kernel, near, group),
        in_specs=[vmem, vmem],
        out_specs=vmem,
        out_shape=jax.ShapeDtypeStruct(held, jnp.float32),
    )(smooth, arrived_y.reshape(held))
    returned = exchange(back.reshape(sent), 2)
    predicted, misfit = pl.pallas_call(
        functools.partial(finish_kernel, near, group),
        in_specs=[vmem],
        out_specs=[vmem, vmem],
        out_shape=[jax.ShapeDtypeStruct((rows, 2, pair_total), jnp.float32),
                   jax.ShapeDtypeStruct((1, 1), jnp.float32)],
    )(returned)
    predicted = predicted.reshape(snap_local, components, height_local, 2, pair_total)
    return (predicted, misfit.reshape(1))


def solution(mesh):
    return jax.shard_map(
        per_device,
        mesh=mesh,
        in_specs=(
            P("snap", None, "height", None, None, None),
            P("snap", None, "height", None, None, None),
            P(),
            P(),
        ),
        out_specs=(P("snap", None, "height", None, None), P()),
        check_vma=False,
    )
```

```python
import functools
import math

import jax
import jax.numpy as jnp
from jax import lax
from jax.experimental import pallas as pl
from jax.experimental.pallas import tpu as pltpu
from jax.sharding import PartitionSpec as P

HIGHEST = lax.Precision.HIGHEST
CHUNK = 8
LANES = 128


def pair_tables(pair_list, points, mode_count):
    grid = jnp.arange(points, dtype=jnp.int32)
    ordered = jnp.repeat(pair_list, 2, axis=0)
    imaginary = (jnp.arange(ordered.shape[0], dtype=jnp.int32) % 2 == 1)[None, :]
    phase = grid[:, None] * ordered[None, :, 1] % points
    theta = phase.astype(jnp.float32) * (2.0 * math.pi / points)
    scaling = 1.0 / math.sqrt(points)
    cosine = jnp.cos(theta) * scaling
    sine = jnp.sin(theta) * scaling
    table = jnp.concatenate(
        [jnp.where(imaginary, -sine, cosine), jnp.where(imaginary, cosine, sine)], axis=1
    ).astype(jnp.bfloat16)
    lines = jnp.arange(2 * mode_count, dtype=jnp.int32)
    chosen = (lines[:, None] // 2) == ordered[None, :, 0]
    even = (lines % 2 == 0)[:, None]
    mask = jnp.concatenate([chosen & even, chosen & ~even], axis=1)
    return table, mask.astype(jnp.float32)


def group_size(snap_local, near):
    group = 1
    while snap_local % (2 * group) == 0 and 2 * group * near <= LANES - 2:
        group *= 2
    return group


def spectrum_kernel(x_ref, table_ref, mask_ref, out_ref, held):
    block, lines, points = x_ref.shape
    columns = out_ref.shape[0]
    held[...] = jnp.zeros_like(held)
    for start in range(0, block, CHUNK):
        rows = x_ref[start:start + CHUNK].reshape(CHUNK * lines, points)
        product = jnp.dot(rows, table_ref[...], preferred_element_type=jnp.float32)
        product = product.reshape(CHUNK, lines, 2 * columns) * mask_ref[...][None]
        both = product[:, :, :columns] + product[:, :, columns:]
        held[start:start + CHUNK, :] = jnp.sum(both, axis=1)
    out_ref[:, pl.ds(pl.program_id(0), 1), :] = held[...].T[:, None, :]


def spectrum(values, table, mask, near, group):
    lines, points = values.shape[1:]
    columns = mask.shape[1] // 2
    block = near * group
    steps = values.shape[0] // block
    return pl.pallas_call(
        spectrum_kernel,
        grid=(steps,),
        in_specs=[pl.BlockSpec((block, lines, points), lambda i: (i, 0, 0)),
                  pl.BlockSpec(table.shape, lambda i: (0, 0)),
                  pl.BlockSpec(mask.shape, lambda i: (0, 0))],
        out_specs=pl.BlockSpec((columns, steps, LANES), lambda i: (0, 0, 0)),
        out_shape=jax.ShapeDtypeStruct((columns, steps, LANES), jnp.float32),
        scratch_shapes=[pltpu.VMEM((LANES, columns), jnp.float32)],
        cost_estimate=pl.CostEstimate(flops=4 * values.size * columns, bytes_accessed=2 * values.size, transcendentals=0),
    )(values, table, mask)


def gather_pair(ref, pair, near, group):
    snap_count, height_count, _, _, steps, _ = ref.shape
    lane = lax.broadcasted_iota(jnp.int32, (1, LANES), 1)
    pieces = []
    for height in range(height_count):
        parts = []
        for half in range(2):
            block = ref[:, height, pair, half].reshape(snap_count * steps, LANES)
            for member in range(group):
                moved = block if member == 0 else pltpu.roll(block, LANES - member * near, 1)
                parts.append(jnp.where(lane < near, moved, 0.0))
        pieces.append(jnp.concatenate(parts, axis=0))
    return jnp.concatenate(pieces, axis=1)


def invert_kernel(near, group, ridge_ref, x_ref, smooth_ref):
    pairs = x_ref.shape[2]
    snaps = smooth_ref.shape[1] // 2
    lane = lax.broadcasted_iota(jnp.int32, (snaps, 2 * snaps), 1)
    line = lax.broadcasted_iota(jnp.int32, (snaps, 2 * snaps), 0)
    sign = jnp.where(lax.broadcasted_iota(jnp.int32, (1, 2 * snaps), 1) < snaps, -1.0, 1.0)

    def embed(top):
        return jnp.concatenate([top, pltpu.roll(top, snaps, 1) * sign], axis=0)

    grams = []
    states = []
    for pair in range(pairs):
        stacked = gather_pair(x_ref, pair, near, group)
        gram = lax.dot_general(stacked, stacked, (((1,), (1,)), ((), ())), precision=HIGHEST,
                               preferred_element_type=jnp.float32)
        swapped = pltpu.roll(gram[snaps:], snaps, 1)
        top = gram[:snaps] + jnp.where(lane < snaps, swapped, 0.0)
        top = jnp.where(lane < snaps, top, swapped - gram[:snaps])
        grams.append(top)
        states.append(top + jnp.where(line == lane, ridge_ref[pair], 0.0))
    turned = [pltpu.roll(state, snaps, 1) * sign for state in states]
    for k in range(snaps):
        here = line == k
        column = (lane == k) | (lane == snaps + k)
        unit = jnp.where(here & (lane == k), 1.0, 0.0)
        other = jnp.where(here & (lane == snaps + k), 1.0, 0.0)
        for pair in range(pairs):
            state, twin = states[pair], turned[pair]
            first = state[:, k:k + 1]
            second = state[:, snaps + k:snaps + k + 1]
            inverse = 1.0 / state[k:k + 1, k:k + 1]
            cleared = jnp.where(column, unit, state)
            cleared_twin = jnp.where(column, other, twin)
            row = cleared[k:k + 1, :] * inverse
            row_twin = cleared_twin[k:k + 1, :] * inverse
            states[pair] = jnp.where(here, row, cleared - (first * row + second * row_twin))
            turned[pair] = jnp.where(here, row_twin, cleared_twin - (first * row_twin - second * row))
    for pair in range(pairs):
        smooth_ref[pair] = jnp.dot(embed(grams[pair]), jnp.concatenate([states[pair], turned[pair]], axis=0), precision=HIGHEST,
                                   preferred_element_type=jnp.float32)


def apply_kernel(near, group, smooth_ref, y_ref, back_ref):
    snap_count, height_count, pairs, _, steps, _ = y_ref.shape
    members = snap_count * steps
    half_rows = group * members
    lane = lax.broadcasted_iota(jnp.int32, (1, LANES), 1)
    misses = jnp.zeros((1, 1), jnp.float32)
    energy = jnp.zeros((1, 1), jnp.float32)
    for pair in range(pairs):
        target = gather_pair(y_ref, pair, near, group)
        fitted = jnp.dot(smooth_ref[pair], target, precision=HIGHEST, preferred_element_type=jnp.float32)
        gap = target - fitted
        misses = misses + jnp.sum(gap * gap, keepdims=True)
        energy = energy + jnp.sum(target * target, keepdims=True)
        note = jnp.where(lane == near * group, misses, jnp.where(lane == near * group + 1, energy, 0.0))
        for height in range(height_count):
            for half in range(2):
                block = jnp.broadcast_to(note, (members, LANES))
                for member in range(group):
                    start = half * half_rows + member * members
                    piece = fitted[start:start + members, height * LANES:(height + 1) * LANES]
                    block = block + (piece if member == 0 else pltpu.roll(piece, member * near, 1))
                back_ref[:, height, pair, half] = block.reshape(snap_count, steps, LANES)


def finish_kernel(near, group, back_ref, predicted_ref, misfit_ref):
    owners, pairs, _, steps, _ = back_ref.shape
    block = near * group
    for half in range(2):
        for step in range(steps):
            sheet = back_ref[:, :, half, step, :].reshape(owners * pairs, LANES)
            predicted_ref[step * block:(step + 1) * block, half, :] = sheet.T[:block]
    notes = jnp.sum(back_ref[:, pairs - 1, 0, 0, :], axis=0, keepdims=True)
    misfit_ref[...] = notes[:, block:block + 1] / notes[:, block + 1:block + 2]


def exchange(message):
    return lax.all_to_all(message, ("snap", "height"), split_axis=0, concat_axis=0, tiled=True)


def scatter_kernel(out_ref, in_ref, send_sem, recv_sem, own_sem):
    owners = out_ref.shape[0]
    height_count = lax.axis_size("height")
    me = lax.axis_index("snap") * height_count + lax.axis_index("height")
    barrier = pltpu.get_barrier_semaphore()

    def peer(step):
        other = lax.rem(me + step, owners)
        return other, (other // height_count, lax.rem(other, height_count))

    def greet(step, carry):
        _, where = peer(step)
        pl.semaphore_signal(barrier, inc=1, device_id=where, device_id_type=pl.DeviceIdType.MESH)
        return carry

    def copy(step):
        other, where = peer(step)
        return pltpu.make_async_remote_copy(
            src_ref=out_ref.at[other],
            dst_ref=in_ref.at[me],
            send_sem=send_sem.at[step],
            recv_sem=recv_sem.at[step],
            device_id=where,
            device_id_type=pl.DeviceIdType.MESH,
        )

    def start(step, carry):
        copy(step).start()
        return carry

    def finish(step, carry):
        copy(step).wait()
        return carry

    own = pltpu.make_async_copy(out_ref.at[me], in_ref.at[me], own_sem)
    own.start()
    lax.fori_loop(1, owners, greet, 0)
    pl.semaphore_wait(barrier, owners - 1)
    lax.fori_loop(1, owners, start, 0)
    lax.fori_loop(1, owners, finish, 0)
    own.wait()


def scatter(message):
    owners = message.shape[0]
    vmem = pl.BlockSpec(memory_space=pltpu.VMEM)
    return pl.pallas_call(
        scatter_kernel,
        in_specs=[vmem],
        out_specs=vmem,
        out_shape=jax.ShapeDtypeStruct(message.shape, message.dtype),
        scratch_shapes=[pltpu.SemaphoreType.DMA((owners,)), pltpu.SemaphoreType.DMA((owners,)),
                        pltpu.SemaphoreType.DMA],
        compiler_params=pltpu.CompilerParams(collective_id=0, has_side_effects=True),
    )(message)


def per_device(resolved, drain, pair_list, ridge_index):
    snap_local, components, height_local, mode_count, halves, points = resolved.shape
    snap_count = lax.axis_size("snap")
    height_count = lax.axis_size("height")
    owners = snap_count * height_count
    pair_total = pair_list.shape[0]
    pair_local = pair_total // owners
    near = components * height_local
    rows = snap_local * near
    snaps = snap_count * snap_local
    group = group_size(snap_local, near)
    steps = snap_local // group
    sent = (owners, pair_local, 2, steps, LANES)
    held = (snap_count, height_count, pair_local, 2, steps, LANES)
    vmem = pl.BlockSpec(memory_space=pltpu.VMEM)
    smem = pl.BlockSpec(memory_space=pltpu.SMEM)

    table, mask = pair_tables(pair_list, points, mode_count)
    spec_x = spectrum(resolved.reshape(rows, -1, points), table, mask, near, group)
    arrived_x = exchange(spec_x.reshape(sent))
    spec_y = spectrum(drain.reshape(rows, -1, points), table, mask, near, group)
    arrived_y = exchange(spec_y.reshape(sent))
    owner_index = lax.axis_index("snap") * height_count + lax.axis_index("height")
    levels = lax.dynamic_slice_in_dim(ridge_index, owner_index * pair_local, pair_local, 0)
    ridge = 0.25 * jnp.exp2(levels.astype(jnp.float32)) * snaps
    smooth = pl.pallas_call(
        functools.partial(invert_kernel, near, group),
        in_specs=[smem, vmem],
        out_specs=vmem,
        out_shape=jax.ShapeDtypeStruct((pair_local, 2 * snaps, 2 * snaps), jnp.float32),
        cost_estimate=pl.CostEstimate(flops=10**10, bytes_accessed=2**20, transcendentals=0),
    )(ridge, arrived_x.reshape(held))
    back = pl.pallas_call(
        functools.partial(apply_kernel, near, group),
        in_specs=[vmem, vmem],
        out_specs=vmem,
        out_shape=jax.ShapeDtypeStruct(held, jnp.float32),
    )(smooth, arrived_y.reshape(held))
    returned = scatter(back.reshape(sent))
    predicted, misfit = pl.pallas_call(
        functools.partial(finish_kernel, near, group),
        in_specs=[vmem],
        out_specs=[vmem, vmem],
        out_shape=[jax.ShapeDtypeStruct((rows, 2, pair_total), jnp.float32),
                   jax.ShapeDtypeStruct((1, 1), jnp.float32)],
    )(returned)
    predicted = predicted.reshape(snap_local, components, height_local, 2, pair_total)
    return (predicted, misfit.reshape(1))


def solution(mesh):
    return jax.shard_map(
        per_device,
        mesh=mesh,
        in_specs=(
            P("snap", None, "height", None, None, None),
            P("snap", None, "height", None, None, None),
            P(),
            P(),
        ),
        out_specs=(P("snap", None, "height", None, None), P()),
        check_vma=False,
    )
```

```python
import functools
import math

import jax
import jax.numpy as jnp
from jax import lax
from jax.experimental import pallas as pl
from jax.experimental.pallas import tpu as pltpu
from jax.sharding import PartitionSpec as P

HIGHEST = lax.Precision.HIGHEST
CHUNK = 8
LANES = 128


def pair_tables(pair_list, points, mode_count):
    grid = jnp.arange(points, dtype=jnp.int32)
    ordered = jnp.repeat(pair_list, 2, axis=0)
    imaginary = (jnp.arange(ordered.shape[0], dtype=jnp.int32) % 2 == 1)[None, :]
    phase = grid[:, None] * ordered[None, :, 1] % points
    theta = phase.astype(jnp.float32) * (2.0 * math.pi / points)
    scaling = 1.0 / math.sqrt(points)
    cosine = jnp.cos(theta) * scaling
    sine = jnp.sin(theta) * scaling
    table = jnp.concatenate(
        [jnp.where(imaginary, -sine, cosine), jnp.where(imaginary, cosine, sine)], axis=1
    ).astype(jnp.bfloat16)
    lines = jnp.arange(2 * mode_count, dtype=jnp.int32)
    chosen = (lines[:, None] // 2) == ordered[None, :, 0]
    even = (lines % 2 == 0)[:, None]
    mask = jnp.concatenate([chosen & even, chosen & ~even], axis=1)
    return table, mask.astype(jnp.float32)


def group_size(snap_local, near):
    group = 1
    while snap_local % (2 * group) == 0 and 2 * group * near <= LANES - 2:
        group *= 2
    return group


def exchange(out_ref, in_ref, send_sem, recv_sem, own_sem):
    owners = out_ref.shape[0]
    height_count = lax.axis_size("height")
    me = lax.axis_index("snap") * height_count + lax.axis_index("height")

    def peer(step):
        other = lax.rem(me + step, owners)
        return other, (other // height_count, lax.rem(other, height_count))

    def greet(step, carry):
        _, where = peer(step)
        pl.semaphore_signal(pltpu.get_barrier_semaphore(), inc=1, device_id=where,
                            device_id_type=pl.DeviceIdType.MESH)
        return carry

    def copy(step):
        other, where = peer(step)
        return pltpu.make_async_remote_copy(
            src_ref=out_ref.at[other],
            dst_ref=in_ref.at[me],
            send_sem=send_sem.at[step],
            recv_sem=recv_sem.at[step],
            device_id=where,
            device_id_type=pl.DeviceIdType.MESH,
        )

    def start(step, carry):
        copy(step).start()
        return carry

    def finish(step, carry):
        copy(step).wait()
        return carry

    own = pltpu.make_async_copy(out_ref.at[me], in_ref.at[me], own_sem)

    def begin():
        own.start()
        lax.fori_loop(1, owners, greet, 0)
        pl.semaphore_wait(pltpu.get_barrier_semaphore(), owners - 1)
        lax.fori_loop(1, owners, start, 0)

    def end():
        lax.fori_loop(1, owners, finish, 0)
        own.wait()

    return begin, end


def exchange_scratch(owners):
    return [pltpu.SemaphoreType.DMA((owners,)), pltpu.SemaphoreType.DMA((owners,)), pltpu.SemaphoreType.DMA]


def scatter_kernel(out_ref, in_ref, *sems):
    begin, end = exchange(out_ref, in_ref, *sems)
    begin()
    end()


def scatter(message):
    vmem = pl.BlockSpec(memory_space=pltpu.VMEM)
    return pl.pallas_call(
        scatter_kernel,
        in_specs=[vmem],
        out_specs=vmem,
        out_shape=jax.ShapeDtypeStruct(message.shape, message.dtype),
        scratch_shapes=exchange_scratch(message.shape[0]),
        compiler_params=pltpu.CompilerParams(collective_id=0, has_side_effects=True),
    )(message)


def spectrum_kernel(x_ref, table_ref, mask_ref, out_ref, held):
    block, lines, points = x_ref.shape
    columns = out_ref.shape[0]
    held[...] = jnp.zeros_like(held)
    for start in range(0, block, CHUNK):
        rows = x_ref[start:start + CHUNK].reshape(CHUNK * lines, points)
        product = jnp.dot(rows, table_ref[...], preferred_element_type=jnp.float32)
        product = product.reshape(CHUNK, lines, 2 * columns) * mask_ref[...][None]
        both = product[:, :, :columns] + product[:, :, columns:]
        held[start:start + CHUNK, :] = jnp.sum(both, axis=1)
    out_ref[:, pl.ds(pl.program_id(0), 1), :] = held[...].T[:, None, :]


def spectrum(values, table, mask, near, group):
    lines, points = values.shape[1:]
    columns = mask.shape[1] // 2
    block = near * group
    steps = values.shape[0] // block
    return pl.pallas_call(
        spectrum_kernel,
        grid=(steps,),
        in_specs=[pl.BlockSpec((block, lines, points), lambda i: (i, 0, 0)),
                  pl.BlockSpec(table.shape, lambda i: (0, 0)),
                  pl.BlockSpec(mask.shape, lambda i: (0, 0))],
        out_specs=pl.BlockSpec((columns, steps, LANES), lambda i: (0, 0, 0)),
        out_shape=jax.ShapeDtypeStruct((columns, steps, LANES), jnp.float32),
        scratch_shapes=[pltpu.VMEM((LANES, columns), jnp.float32)],
        cost_estimate=pl.CostEstimate(flops=4 * values.size * columns, bytes_accessed=2 * values.size, transcendentals=0),
    )(values, table, mask)


def spectrum_exchange_kernel(x_ref, table_ref, mask_ref, message_ref, out_ref, arrived_ref, held, *sems):
    begin, end = exchange(message_ref, arrived_ref, *sems)
    step = pl.program_id(0)
    pl.when(step == 0)(begin)
    spectrum_kernel(x_ref, table_ref, mask_ref, out_ref, held)
    pl.when(step == pl.num_programs(0) - 1)(end)


def spectrum_exchange(values, table, mask, near, group, message):
    lines, points = values.shape[1:]
    columns = mask.shape[1] // 2
    block = near * group
    steps = values.shape[0] // block
    anywhere = pl.BlockSpec(memory_space=pl.ANY)
    return pl.pallas_call(
        spectrum_exchange_kernel,
        grid=(steps,),
        in_specs=[pl.BlockSpec((block, lines, points), lambda i: (i, 0, 0)),
                  pl.BlockSpec(table.shape, lambda i: (0, 0)),
                  pl.BlockSpec(mask.shape, lambda i: (0, 0)), anywhere],
        out_specs=[pl.BlockSpec((columns, steps, LANES), lambda i: (0, 0, 0)), anywhere],
        out_shape=[jax.ShapeDtypeStruct((columns, steps, LANES), jnp.float32),
                   jax.ShapeDtypeStruct(message.shape, jnp.float32)],
        scratch_shapes=[pltpu.VMEM((LANES, columns), jnp.float32)] + exchange_scratch(message.shape[0]),
        compiler_params=pltpu.CompilerParams(collective_id=1, has_side_effects=True),
    )(values, table, mask, message)


def gather_pair(ref, pair, near, group):
    snap_count, height_count, _, _, steps, _ = ref.shape
    lane = lax.broadcasted_iota(jnp.int32, (1, LANES), 1)
    pieces = []
    for height in range(height_count):
        parts = []
        for half in range(2):
            block = ref[:, height, pair, half].reshape(snap_count * steps, LANES)
            for member in range(group):
                moved = block if member == 0 else pltpu.roll(block, LANES - member * near, 1)
                parts.append(jnp.where(lane < near, moved, 0.0))
        pieces.append(jnp.concatenate(parts, axis=0))
    return jnp.concatenate(pieces, axis=1)


def invert_kernel(near, group, ridge_ref, x_ref, smooth_ref):
    pairs = x_ref.shape[2]
    snaps = smooth_ref.shape[1] // 2
    lane = lax.broadcasted_iota(jnp.int32, (snaps, 2 * snaps), 1)
    line = lax.broadcasted_iota(jnp.int32, (snaps, 2 * snaps), 0)
    sign = jnp.where(lax.broadcasted_iota(jnp.int32, (1, 2 * snaps), 1) < snaps, -1.0, 1.0)

    def embed(top):
        return jnp.concatenate([top, pltpu.roll(top, snaps, 1) * sign], axis=0)

    grams = []
    states = []
    for pair in range(pairs):
        stacked = gather_pair(x_ref, pair, near, group)
        gram = lax.dot_general(stacked, stacked, (((1,), (1,)), ((), ())), precision=HIGHEST,
                               preferred_element_type=jnp.float32)
        swapped = pltpu.roll(gram[snaps:], snaps, 1)
        top = gram[:snaps] + jnp.where(lane < snaps, swapped, 0.0)
        top = jnp.where(lane < snaps, top, swapped - gram[:snaps])
        grams.append(top)
        states.append(top + jnp.where(line == lane, ridge_ref[pair], 0.0))
    turned = [pltpu.roll(state, snaps, 1) * sign for state in states]
    for k in range(snaps):
        here = line == k
        column = (lane == k) | (lane == snaps + k)
        unit = jnp.where(here & (lane == k), 1.0, 0.0)
        other = jnp.where(here & (lane == snaps + k), 1.0, 0.0)
        for pair in range(pairs):
            state, twin = states[pair], turned[pair]
            first = state[:, k:k + 1]
            second = state[:, snaps + k:snaps + k + 1]
            inverse = 1.0 / state[k:k + 1, k:k + 1]
            cleared = jnp.where(column, unit, state)
            cleared_twin = jnp.where(column, other, twin)
            row = cleared[k:k + 1, :] * inverse
            row_twin = cleared_twin[k:k + 1, :] * inverse
            states[pair] = jnp.where(here, row, cleared - (first * row + second * row_twin))
            turned[pair] = jnp.where(here, row_twin, cleared_twin - (first * row_twin - second * row))
    for pair in range(pairs):
        smooth_ref[pair] = jnp.dot(embed(grams[pair]), jnp.concatenate([states[pair], turned[pair]], axis=0), precision=HIGHEST,
                                   preferred_element_type=jnp.float32)


def invert_exchange_kernel(near, group, ridge_ref, x_ref, message_ref, smooth_ref, arrived_ref, *sems):
    begin, end = exchange(message_ref, arrived_ref, *sems)
    begin()
    invert_kernel(near, group, ridge_ref, x_ref, smooth_ref)
    end()


def apply_kernel(near, group, smooth_ref, y_ref, back_ref):
    snap_count, height_count, pairs, _, steps, _ = y_ref.shape
    members = snap_count * steps
    half_rows = group * members
    lane = lax.broadcasted_iota(jnp.int32, (1, LANES), 1)
    misses = jnp.zeros((1, 1), jnp.float32)
    energy = jnp.zeros((1, 1), jnp.float32)
    for pair in range(pairs):
        target = gather_pair(y_ref, pair, near, group)
        fitted = jnp.dot(smooth_ref[pair], target, precision=HIGHEST, preferred_element_type=jnp.float32)
        gap = target - fitted
        misses = misses + jnp.sum(gap * gap, keepdims=True)
        energy = energy + jnp.sum(target * target, keepdims=True)
        note = jnp.where(lane == near * group, misses, jnp.where(lane == near * group + 1, energy, 0.0))
        for height in range(height_count):
            for half in range(2):
                block = jnp.broadcast_to(note, (members, LANES))
                for member in range(group):
                    start = half * half_rows + member * members
                    piece = fitted[start:start + members, height * LANES:(height + 1) * LANES]
                    block = block + (piece if member == 0 else pltpu.roll(piece, member * near, 1))
                back_ref[:, height, pair, half] = block.reshape(snap_count, steps, LANES)


def finish_kernel(near, group, back_ref, predicted_ref, misfit_ref):
    owners, pairs, _, steps, _ = back_ref.shape
    block = near * group
    for half in range(2):
        for step in range(steps):
            sheet = back_ref[:, :, half, step, :].reshape(owners * pairs, LANES)
            predicted_ref[step * block:(step + 1) * block, half, :] = sheet.T[:block]
    notes = jnp.sum(back_ref[:, pairs - 1, 0, 0, :], axis=0, keepdims=True)
    misfit_ref[...] = notes[:, block:block + 1] / notes[:, block + 1:block + 2]


def per_device(resolved, drain, pair_list, ridge_index):
    snap_local, components, height_local, mode_count, halves, points = resolved.shape
    snap_count = lax.axis_size("snap")
    height_count = lax.axis_size("height")
    owners = snap_count * height_count
    pair_total = pair_list.shape[0]
    pair_local = pair_total // owners
    near = components * height_local
    rows = snap_local * near
    snaps = snap_count * snap_local
    group = group_size(snap_local, near)
    steps = snap_local // group
    sent = (owners, pair_local, 2, steps, LANES)
    held = (snap_count, height_count, pair_local, 2, steps, LANES)
    vmem = pl.BlockSpec(memory_space=pltpu.VMEM)
    smem = pl.BlockSpec(memory_space=pltpu.SMEM)

    table, mask = pair_tables(pair_list, points, mode_count)
    spec_x = spectrum(resolved.reshape(rows, -1, points), table, mask, near, group)
    spec_y, arrived_x = spectrum_exchange(
        drain.reshape(rows, -1, points), table, mask, near, group, spec_x.reshape(sent)
    )
    owner_index = lax.axis_index("snap") * height_count + lax.axis_index("height")
    levels = lax.dynamic_slice_in_dim(ridge_index, owner_index * pair_local, pair_local, 0)
    ridge = 0.25 * jnp.exp2(levels.astype(jnp.float32)) * snaps
    anywhere = pl.BlockSpec(memory_space=pl.ANY)
    smooth, arrived_y = pl.pallas_call(
        functools.partial(invert_exchange_kernel, near, group),
        in_specs=[smem, vmem, anywhere],
        out_specs=[vmem, anywhere],
        out_shape=[jax.ShapeDtypeStruct((pair_local, 2 * snaps, 2 * snaps), jnp.float32),
                   jax.ShapeDtypeStruct(sent, jnp.float32)],
        scratch_shapes=exchange_scratch(owners),
        compiler_params=pltpu.CompilerParams(collective_id=2, has_side_effects=True),
    )(ridge, arrived_x.reshape(held), spec_y.reshape(sent))
    back = pl.pallas_call(
        functools.partial(apply_kernel, near, group),
        in_specs=[vmem, vmem],
        out_specs=vmem,
        out_shape=jax.ShapeDtypeStruct(held, jnp.float32),
    )(smooth, arrived_y.reshape(held))
    returned = scatter(back.reshape(sent))
    predicted, misfit = pl.pallas_call(
        functools.partial(finish_kernel, near, group),
        in_specs=[vmem],
        out_specs=[vmem, vmem],
        out_shape=[jax.ShapeDtypeStruct((rows, 2, pair_total), jnp.float32),
                   jax.ShapeDtypeStruct((1, 1), jnp.float32)],
    )(returned)
    predicted = predicted.reshape(snap_local, components, height_local, 2, pair_total)
    return (predicted, misfit.reshape(1))


def solution(mesh):
    return jax.shard_map(
        per_device,
        mesh=mesh,
        in_specs=(
            P("snap", None, "height", None, None, None),
            P("snap", None, "height", None, None, None),
            P(),
            P(),
        ),
        out_specs=(P("snap", None, "height", None, None), P()),
        check_vma=False,
    )
```

```python
import functools
import math

import jax
import jax.numpy as jnp
from jax import lax
from jax.experimental import pallas as pl
from jax.experimental.pallas import tpu as pltpu
from jax.sharding import PartitionSpec as P

HIGHEST = lax.Precision.HIGHEST
CHUNK = 8
LANES = 128


def pair_tables(pair_list, points, mode_count):
    grid = jnp.arange(points, dtype=jnp.int32)
    ordered = jnp.repeat(pair_list, 2, axis=0)
    imaginary = (jnp.arange(ordered.shape[0], dtype=jnp.int32) % 2 == 1)[None, :]
    phase = grid[:, None] * ordered[None, :, 1] % points
    theta = phase.astype(jnp.float32) * (2.0 * math.pi / points)
    scaling = 1.0 / math.sqrt(points)
    cosine = jnp.cos(theta) * scaling
    sine = jnp.sin(theta) * scaling
    table = jnp.concatenate(
        [jnp.where(imaginary, -sine, cosine), jnp.where(imaginary, cosine, sine)], axis=1
    ).astype(jnp.bfloat16)
    lines = jnp.arange(2 * mode_count, dtype=jnp.int32)
    chosen = (lines[:, None] // 2) == ordered[None, :, 0]
    even = (lines % 2 == 0)[:, None]
    mask = jnp.concatenate([chosen & even, chosen & ~even], axis=1)
    return table, mask.astype(jnp.float32)


def group_size(snap_local, near):
    group = 1
    while snap_local % (2 * group) == 0 and 2 * group * near <= LANES - 2:
        group *= 2
    return group


def exchange(out_ref, in_ref, send_sem, recv_sem, own_sem):
    owners = out_ref.shape[0]
    height_count = lax.axis_size("height")
    me = lax.axis_index("snap") * height_count + lax.axis_index("height")

    stride = height_count + 1 if math.gcd(height_count + 1, owners) == 1 else 1

    def peer(step):
        other = lax.rem(me + step * stride, owners)
        return other, (other // height_count, lax.rem(other, height_count))

    def greet(step, carry):
        _, where = peer(step)
        pl.semaphore_signal(pltpu.get_barrier_semaphore(), inc=1, device_id=where,
                            device_id_type=pl.DeviceIdType.MESH)
        return carry

    def copy(step):
        other, where = peer(step)
        return pltpu.make_async_remote_copy(
            src_ref=out_ref.at[other],
            dst_ref=in_ref.at[me],
            send_sem=send_sem.at[step],
            recv_sem=recv_sem.at[step],
            device_id=where,
            device_id_type=pl.DeviceIdType.MESH,
        )

    def start(step, carry):
        copy(step).start()
        return carry

    def finish(step, carry):
        copy(step).wait()
        return carry

    own = pltpu.make_async_copy(out_ref.at[me], in_ref.at[me], own_sem)

    def begin():
        own.start()
        lax.fori_loop(1, owners, greet, 0)
        pl.semaphore_wait(pltpu.get_barrier_semaphore(), owners - 1)
        lax.fori_loop(1, owners, start, 0)

    def end():
        lax.fori_loop(1, owners, finish, 0)
        own.wait()

    return begin, end


def exchange_scratch(owners):
    return [pltpu.SemaphoreType.DMA((owners,)), pltpu.SemaphoreType.DMA((owners,)), pltpu.SemaphoreType.DMA]


def scatter_kernel(out_ref, in_ref, *sems):
    begin, end = exchange(out_ref, in_ref, *sems)
    begin()
    end()


def scatter(message):
    vmem = pl.BlockSpec(memory_space=pltpu.VMEM)
    return pl.pallas_call(
        scatter_kernel,
        in_specs=[vmem],
        out_specs=vmem,
        out_shape=jax.ShapeDtypeStruct(message.shape, message.dtype),
        scratch_shapes=exchange_scratch(message.shape[0]),
        compiler_params=pltpu.CompilerParams(collective_id=0, has_side_effects=True),
    )(message)


def spectrum_kernel(x_ref, table_ref, mask_ref, out_ref, held):
    block, lines, points = x_ref.shape
    columns = out_ref.shape[0]
    held[...] = jnp.zeros_like(held)
    for start in range(0, block, CHUNK):
        rows = x_ref[start:start + CHUNK].reshape(CHUNK * lines, points)
        product = jnp.dot(rows, table_ref[...], preferred_element_type=jnp.float32)
        product = product.reshape(CHUNK, lines, 2 * columns) * mask_ref[...][None]
        both = product[:, :, :columns] + product[:, :, columns:]
        held[start:start + CHUNK, :] = jnp.sum(both, axis=1)
    out_ref[:, pl.ds(pl.program_id(0), 1), :] = held[...].T[:, None, :]


def spectrum(values, table, mask, near, group):
    lines, points = values.shape[1:]
    columns = mask.shape[1] // 2
    block = near * group
    steps = values.shape[0] // block
    return pl.pallas_call(
        spectrum_kernel,
        grid=(steps,),
        in_specs=[pl.BlockSpec((block, lines, points), lambda i: (i, 0, 0)),
                  pl.BlockSpec(table.shape, lambda i: (0, 0)),
                  pl.BlockSpec(mask.shape, lambda i: (0, 0))],
        out_specs=pl.BlockSpec((columns, steps, LANES), lambda i: (0, 0, 0)),
        out_shape=jax.ShapeDtypeStruct((columns, steps, LANES), jnp.float32),
        scratch_shapes=[pltpu.VMEM((LANES, columns), jnp.float32)],
        cost_estimate=pl.CostEstimate(flops=4 * values.size * columns, bytes_accessed=2 * values.size, transcendentals=0),
    )(values, table, mask)


def spectrum_exchange_kernel(x_ref, table_ref, mask_ref, message_ref, out_ref, arrived_ref, held, *sems):
    begin, end = exchange(message_ref, arrived_ref, *sems)
    step = pl.program_id(0)
    pl.when(step == 0)(begin)
    spectrum_kernel(x_ref, table_ref, mask_ref, out_ref, held)
    pl.when(step == pl.num_programs(0) - 1)(end)


def spectrum_exchange(values, table, mask, near, group, message):
    lines, points = values.shape[1:]
    columns = mask.shape[1] // 2
    block = near * group
    steps = values.shape[0] // block
    anywhere = pl.BlockSpec(memory_space=pl.ANY)
    return pl.pallas_call(
        spectrum_exchange_kernel,
        grid=(steps,),
        in_specs=[pl.BlockSpec((block, lines, points), lambda i: (i, 0, 0)),
                  pl.BlockSpec(table.shape, lambda i: (0, 0)),
                  pl.BlockSpec(mask.shape, lambda i: (0, 0)), anywhere],
        out_specs=[pl.BlockSpec((columns, steps, LANES), lambda i: (0, 0, 0)), anywhere],
        out_shape=[jax.ShapeDtypeStruct((columns, steps, LANES), jnp.float32),
                   jax.ShapeDtypeStruct(message.shape, jnp.float32)],
        scratch_shapes=[pltpu.VMEM((LANES, columns), jnp.float32)] + exchange_scratch(message.shape[0]),
        compiler_params=pltpu.CompilerParams(collective_id=1, has_side_effects=True),
    )(values, table, mask, message)


def gather_pair(ref, pair, near, group):
    snap_count, height_count, _, _, steps, _ = ref.shape
    lane = lax.broadcasted_iota(jnp.int32, (1, LANES), 1)
    pieces = []
    for height in range(height_count):
        parts = []
        for half in range(2):
            block = ref[:, height, pair, half].reshape(snap_count * steps, LANES)
            for member in range(group):
                moved = block if member == 0 else pltpu.roll(block, LANES - member * near, 1)
                parts.append(jnp.where(lane < near, moved, 0.0))
        pieces.append(jnp.concatenate(parts, axis=0))
    return jnp.concatenate(pieces, axis=1)


def invert_kernel(near, group, ridge_ref, x_ref, smooth_ref):
    pairs = x_ref.shape[2]
    snaps = smooth_ref.shape[1] // 2
    lane = lax.broadcasted_iota(jnp.int32, (snaps, 2 * snaps), 1)
    line = lax.broadcasted_iota(jnp.int32, (snaps, 2 * snaps), 0)
    sign = jnp.where(lax.broadcasted_iota(jnp.int32, (1, 2 * snaps), 1) < snaps, -1.0, 1.0)

    def embed(top):
        return jnp.concatenate([top, pltpu.roll(top, snaps, 1) * sign], axis=0)

    grams = []
    states = []
    for pair in range(pairs):
        stacked = gather_pair(x_ref, pair, near, group)
        gram = lax.dot_general(stacked, stacked, (((1,), (1,)), ((), ())), precision=HIGHEST,
                               preferred_element_type=jnp.float32)
        swapped = pltpu.roll(gram[snaps:], snaps, 1)
        top = gram[:snaps] + jnp.where(lane < snaps, swapped, 0.0)
        top = jnp.where(lane < snaps, top, swapped - gram[:snaps])
        grams.append(top)
        states.append(top + jnp.where(line == lane, ridge_ref[pair], 0.0))
    turned = [pltpu.roll(state, snaps, 1) * sign for state in states]
    for k in range(snaps):
        here = line == k
        column = (lane == k) | (lane == snaps + k)
        unit = jnp.where(here & (lane == k), 1.0, 0.0)
        other = jnp.where(here & (lane == snaps + k), 1.0, 0.0)
        for pair in range(pairs):
            state, twin = states[pair], turned[pair]
            first = state[:, k:k + 1]
            second = state[:, snaps + k:snaps + k + 1]
            inverse = 1.0 / state[k:k + 1, k:k + 1]
            cleared = jnp.where(column, unit, state)
            cleared_twin = jnp.where(column, other, twin)
            row = cleared[k:k + 1, :] * inverse
            row_twin = cleared_twin[k:k + 1, :] * inverse
            states[pair] = jnp.where(here, row, cleared - (first * row + second * row_twin))
            turned[pair] = jnp.where(here, row_twin, cleared_twin - (first * row_twin - second * row))
    for pair in range(pairs):
        smooth_ref[pair] = jnp.dot(embed(grams[pair]), jnp.concatenate([states[pair], turned[pair]], axis=0), precision=HIGHEST,
                                   preferred_element_type=jnp.float32)


def invert_exchange_kernel(near, group, ridge_ref, x_ref, message_ref, smooth_ref, arrived_ref, *sems):
    begin, end = exchange(message_ref, arrived_ref, *sems)
    begin()
    invert_kernel(near, group, ridge_ref, x_ref, smooth_ref)
    end()


def apply_kernel(near, group, smooth_ref, y_ref, back_ref):
    snap_count, height_count, pairs, _, steps, _ = y_ref.shape
    members = snap_count * steps
    half_rows = group * members
    lane = lax.broadcasted_iota(jnp.int32, (1, LANES), 1)
    misses = jnp.zeros((1, 1), jnp.float32)
    energy = jnp.zeros((1, 1), jnp.float32)
    for pair in range(pairs):
        target = gather_pair(y_ref, pair, near, group)
        fitted = jnp.dot(smooth_ref[pair], target, precision=HIGHEST, preferred_element_type=jnp.float32)
        gap = target - fitted
        misses = misses + jnp.sum(gap * gap, keepdims=True)
        energy = energy + jnp.sum(target * target, keepdims=True)
        note = jnp.where(lane == near * group, misses, jnp.where(lane == near * group + 1, energy, 0.0))
        for height in range(height_count):
            for half in range(2):
                block = jnp.broadcast_to(note, (members, LANES))
                for member in range(group):
                    start = half * half_rows + member * members
                    piece = fitted[start:start + members, height * LANES:(height + 1) * LANES]
                    block = block + (piece if member == 0 else pltpu.roll(piece, member * near, 1))
                back_ref[:, height, pair, half] = block.reshape(snap_count, steps, LANES)


def finish_kernel(near, group, back_ref, predicted_ref, misfit_ref):
    owners, pairs, _, steps, _ = back_ref.shape
    block = near * group
    for half in range(2):
        for step in range(steps):
            sheet = back_ref[:, :, half, step, :].reshape(owners * pairs, LANES)
            predicted_ref[step * block:(step + 1) * block, half, :] = sheet.T[:block]
    notes = jnp.sum(back_ref[:, pairs - 1, 0, 0, :], axis=0, keepdims=True)
    misfit_ref[...] = notes[:, block:block + 1] / notes[:, block + 1:block + 2]


def per_device(resolved, drain, pair_list, ridge_index):
    snap_local, components, height_local, mode_count, halves, points = resolved.shape
    snap_count = lax.axis_size("snap")
    height_count = lax.axis_size("height")
    owners = snap_count * height_count
    pair_total = pair_list.shape[0]
    pair_local = pair_total // owners
    near = components * height_local
    rows = snap_local * near
    snaps = snap_count * snap_local
    group = group_size(snap_local, near)
    steps = snap_local // group
    sent = (owners, pair_local, 2, steps, LANES)
    held = (snap_count, height_count, pair_local, 2, steps, LANES)
    vmem = pl.BlockSpec(memory_space=pltpu.VMEM)
    smem = pl.BlockSpec(memory_space=pltpu.SMEM)

    table, mask = pair_tables(pair_list, points, mode_count)
    spec_x = spectrum(resolved.reshape(rows, -1, points), table, mask, near, group)
    spec_y, arrived_x = spectrum_exchange(
        drain.reshape(rows, -1, points), table, mask, near, group, spec_x.reshape(sent)
    )
    owner_index = lax.axis_index("snap") * height_count + lax.axis_index("height")
    levels = lax.dynamic_slice_in_dim(ridge_index, owner_index * pair_local, pair_local, 0)
    ridge = 0.25 * jnp.exp2(levels.astype(jnp.float32)) * snaps
    anywhere = pl.BlockSpec(memory_space=pl.ANY)
    smooth, arrived_y = pl.pallas_call(
        functools.partial(invert_exchange_kernel, near, group),
        in_specs=[smem, vmem, anywhere],
        out_specs=[vmem, anywhere],
        out_shape=[jax.ShapeDtypeStruct((pair_local, 2 * snaps, 2 * snaps), jnp.float32),
                   jax.ShapeDtypeStruct(sent, jnp.float32)],
        scratch_shapes=exchange_scratch(owners),
        compiler_params=pltpu.CompilerParams(collective_id=2, has_side_effects=True),
    )(ridge, arrived_x.reshape(held), spec_y.reshape(sent))
    back = pl.pallas_call(
        functools.partial(apply_kernel, near, group),
        in_specs=[vmem, vmem],
        out_specs=vmem,
        out_shape=jax.ShapeDtypeStruct(held, jnp.float32),
    )(smooth, arrived_y.reshape(held))
    returned = scatter(back.reshape(sent))
    predicted, misfit = pl.pallas_call(
        functools.partial(finish_kernel, near, group),
        in_specs=[vmem],
        out_specs=[vmem, vmem],
        out_shape=[jax.ShapeDtypeStruct((rows, 2, pair_total), jnp.float32),
                   jax.ShapeDtypeStruct((1, 1), jnp.float32)],
    )(returned)
    predicted = predicted.reshape(snap_local, components, height_local, 2, pair_total)
    return (predicted, misfit.reshape(1))


def solution(mesh):
    return jax.shard_map(
        per_device,
        mesh=mesh,
        in_specs=(
            P("snap", None, "height", None, None, None),
            P("snap", None, "height", None, None, None),
            P(),
            P(),
        ),
        out_specs=(P("snap", None, "height", None, None), P()),
        check_vma=False,
    )
```
